32 devices in a mesh: grp: 2 (over y), tm: 4 (over z), chan: 4 (over x, core).
Axes of the slice: x: 2, y: 2, z: 4, core: 2. Of those that a mesh axis runs over, the one named last changes fastest.
Arguments:
- voltages: int32 [512, 65536], P(('grp', 'chan'), 'tm'), parts along dimension 0, may hold values from -128 to 127
- beam_delays: int32 [256, 256], replicated, may hold values from 0 to 4095
- cal_gains: float32 [2, 4096, 256], P(None, ('grp', 'tm', 'chan')), parts along dimension 1, may hold values from -4 to 4
Outputs:
- visibilities: bfloat16 [2, 4096, 256, 256], P(None, ('grp', 'tm', 'chan')), parts along dimension 1
- beam_power: bfloat16 [4096, 16, 256], P(('grp', 'tm', 'chan')), parts along dimension 0
The draws below stay inside these ranges and needn't reach their ends.
There are 2 independent parts, one for each index of `grp`. The reference program is written for one: setup_inputs(seed, part) draws one part's arguments, and reference() takes and returns one part's arrays. A program takes and returns all parts, laid end to end along the dimension named above; an argument that names none is the same for every part. Nothing has to cross between parts.
All inputs are finite; a program needn't handle non-finite values.
Results may differ from the reference program's by a relative error of at most 0.0062.
Values may be sent and summed in bfloat16 or wider, within the bound.
A program may use at most 192 MiB of HBM per device.

```python
import math
import jax
import jax.numpy as jnp
from jax import lax

INP = 256
BEAMS = 256
TAPS = 4
SPEC_DEV = 4
NFFT = 4096
CH = 2048
SAMPLES = 65536
N_TM = 4


def plant(values, key, low, high):
    shape = values.shape
    place = [jax.random.randint(jax.random.fold_in(key, axis), (), 0, shape[axis]) for axis in range(len(shape))]
    values = values.at[tuple(place)].set(low)
    longest = shape.index(max(shape))
    place[longest] = (place[longest] + 1) % shape[longest]
    return values.at[tuple(place)].set(high)


def shard_levels(rng, shape, pieces, low, high):
    def one(axis_at, blocks):
        heights = jax.random.uniform(jax.random.fold_in(jax.random.fold_in(rng, 6), axis_at), (blocks,), jnp.float32, low / len(pieces), high / len(pieces))
        return jnp.repeat(jnp.exp(heights), shape[axis_at] // blocks).reshape((-1,) + (1,) * (len(shape) - axis_at - 1))

    factor_of = one(*pieces[0])
    for cut in pieces[1:]:
        factor_of = factor_of * one(*cut)
    return factor_of


def noise(rng, extent, deviation, bound, pieces=(), kind=jnp.bfloat16):
    values = deviation * jax.random.normal(rng, extent, jnp.float32)
    if pieces:
        values = values * shard_levels(rng, extent, pieces, -0.22, 0.18)
    return jnp.clip(values, -bound, bound).astype(kind)


def setup_inputs(seed: int = 0, part: int = 0) -> dict:
    key_list = jax.random.split(jax.random.key(seed), 4)
    own_keys = jax.random.split(jax.random.fold_in(key_list[3], part), 4)
    voltages = plant(jax.random.randint(own_keys[0], (INP, SAMPLES), -128, 128), jax.random.fold_in(own_keys[0], 1), -128, 127).astype(jnp.int32)
    beam_delays = plant(jax.random.randint(key_list[1], (BEAMS, INP), 0, NFFT), jax.random.fold_in(key_list[1], 1), 0, NFFT - 1).astype(jnp.int32)
    cal_gains = noise(own_keys[2], (2, CH, INP), 0.7, 4.0, ((1, 16),), jnp.float32)
    return dict(voltages=voltages, beam_delays=beam_delays, cal_gains=cal_gains)


def pfb_window():
    total_len = TAPS * NFFT
    sample_pos = jnp.arange(total_len, dtype=jnp.float32)
    centre = (sample_pos - total_len / 2 + 0.5) / NFFT
    taper_win = 0.5 - 0.5 * jnp.cos(2.0 * math.pi * (sample_pos + 0.5) / total_len)
    coeffs = jnp.sinc(centre) * taper_win
    coeffs = coeffs / jnp.sqrt(jnp.sum(coeffs * coeffs))
    return coeffs.reshape(TAPS, NFFT)

def reference(voltages, beam_delays, cal_gains):
    spectra_total = SPEC_DEV * N_TM
    coeffs = pfb_window()
    samples = voltages.astype(jnp.float32).reshape(INP, spectra_total, NFFT)
    padded = jnp.concatenate([samples, jnp.zeros((INP, TAPS - 1, NFFT), jnp.float32)], axis=1)
    in_block = 16
    padded = padded.reshape(INP // in_block, in_block, spectra_total + TAPS - 1, NFFT)

    def channelize(block_in):
        filtered = coeffs[0] * block_in[:, 0:spectra_total]
        for tap_index in range(1, TAPS):
            filtered = filtered + coeffs[tap_index] * block_in[:, tap_index:tap_index + spectra_total]
        freq = jnp.fft.rfft(filtered, axis=-1)[..., :CH] * (1.0 / 64.0)
        return (jnp.real(freq).astype(jnp.bfloat16), jnp.imag(freq).astype(jnp.bfloat16))
    spec_re, spec_im = lax.map(channelize, padded)
    spec_re = spec_re.reshape(INP, spectra_total, CH).transpose(2, 1, 0)
    spec_im = spec_im.reshape(INP, spectra_total, CH).transpose(2, 1, 0)
    ch_block = 64
    n_blocks = CH // ch_block
    chan_index = jnp.arange(CH, dtype=jnp.int32).reshape(n_blocks, ch_block)
    weight_norm = 1.0 / math.sqrt(INP)

    def correlate(packed):
        z_re, z_im, g_re, g_im, chan_ids = packed
        a_re = z_re.astype(jnp.float32)
        a_im = z_im.astype(jnp.float32)
        g_re = g_re[:, None, :]
        g_im = g_im[:, None, :]
        cal_re = (g_re * a_re - g_im * a_im).astype(jnp.bfloat16).astype(jnp.float32)
        cal_im = (g_re * a_im + g_im * a_re).astype(jnp.bfloat16).astype(jnp.float32)
        stacked = jnp.concatenate([cal_re, cal_im], axis=1)
        flipped = jnp.concatenate([cal_im, -cal_re], axis=1)
        vis_re = jnp.einsum('ctp,ctq->cpq', stacked, stacked)
        vis_im = jnp.einsum('ctp,ctq->cpq', flipped, stacked)
        vis_out = (jnp.stack([vis_re, vis_im]) / spectra_total).astype(jnp.bfloat16)
        phase_idx = beam_delays[None, :, :] * chan_ids[:, None, None] % NFFT
        angles = phase_idx.astype(jnp.float32) * (2.0 * math.pi / NFFT)
        weight_re = (jnp.cos(angles) * weight_norm).astype(jnp.bfloat16).astype(jnp.float32)
        weight_im = (-jnp.sin(angles) * weight_norm).astype(jnp.bfloat16).astype(jnp.float32)
        beam_re = jnp.einsum('cti,cbi->ctb', cal_re, weight_re) - jnp.einsum('cti,cbi->ctb', cal_im, weight_im)
        beam_im = jnp.einsum('cti,cbi->ctb', cal_im, weight_re) + jnp.einsum('cti,cbi->ctb', cal_re, weight_im)
        power_out = (beam_re * beam_re + beam_im * beam_im).astype(jnp.bfloat16)
        return (vis_out, power_out)
    vis_all, power_all = lax.map(correlate, (spec_re.reshape(n_blocks, ch_block, spectra_total, INP), spec_im.reshape(n_blocks, ch_block, spectra_total, INP), cal_gains[0].reshape(n_blocks, ch_block, INP), cal_gains[1].reshape(n_blocks, ch_block, INP), chan_index))
    visibilities = vis_all.transpose(1, 0, 2, 3, 4).reshape(2, CH, INP, INP)
    beam_power = power_all.reshape(CH, spectra_total, BEAMS)
    return (visibilities, beam_power)
```

```python
import functools
import math

import jax
import jax.numpy as jnp
import numpy as np
from jax import lax
from jax.experimental import pallas as pl
from jax.experimental.pallas import tpu as pltpu
from jax.sharding import PartitionSpec as P

TAPS = 4
FA = 64
FB = 64
NFFT = 4096
CH = 2048


def shifted(block, axis, distance):
    devices = range(lax.axis_size(axis))
    route = [(i - distance, i) for i in devices if i - distance in devices]
    return lax.ppermute(block, axis, route)


def pfb_window():
    total_len = TAPS * NFFT
    sample_pos = jnp.arange(total_len, dtype=jnp.float32)
    centre = (sample_pos - total_len / 2 + 0.5) / NFFT
    taper_win = 0.5 - 0.5 * jnp.cos(2.0 * math.pi * (sample_pos + 0.5) / total_len)
    coeffs = jnp.sinc(centre) * taper_win
    coeffs = coeffs / jnp.sqrt(jnp.sum(coeffs * coeffs))
    return coeffs.reshape(TAPS, NFFT)


RADIX = 32
LANES = NFFT // RADIX


def real_dft(rows):
    size = len(rows)
    if size == 2:
        return [(rows[0] + rows[1], None), (rows[0] - rows[1], None)]
    even, odd = real_dft(rows[0::2]), real_dft(rows[1::2])
    bins = [None] * (size // 2 + 1)
    bins[0] = (even[0][0] + odd[0][0], None)
    bins[size // 2] = (even[0][0] - odd[0][0], None)
    for k in range(1, size // 4):
        cos, sin = math.cos(2 * math.pi * k / size), math.sin(2 * math.pi * k / size)
        o_re, o_im = odd[k]
        t_re = o_re * cos + o_im * sin
        t_im = o_im * cos - o_re * sin
        bins[k] = (even[k][0] + t_re, even[k][1] + t_im)
        bins[size // 2 - k] = (even[k][0] - t_re, t_im - even[k][1])
    bins[size // 4] = (even[size // 4][0], -odd[size // 4][0])
    return bins


def twiddles():
    angle = 2.0 * np.pi * np.outer(np.arange(RADIX // 2 + 1), np.arange(LANES)) / NFFT
    table = np.stack([np.cos(angle), np.sin(angle)], axis=1).astype(np.float32)
    return np.broadcast_to(table[:, :, None, :], table.shape[:2] + (8, LANES))


def second_stage(groups):
    half = LANES // 2
    q = np.arange(LANES)
    angle = 2.0 * np.pi * (np.outer(q, q) % LANES) / LANES
    cos, sin = np.cos(angle) / 64.0, np.sin(angle) / 64.0
    real = np.concatenate([cos, sin], axis=1)
    imag = np.concatenate([-sin, cos], axis=1)
    plain = np.stack([real[:half], imag[:half]])
    mirror = np.stack([real[::-1][:half], -imag[::-1][:half]])
    none = np.zeros_like(plain)

    def ordered(first, second):
        rows = np.stack([first, second]).reshape(2, 2, groups, half // groups, 2 * LANES)
        return rows.transpose(2, 0, 1, 3, 4).reshape(2 * LANES, 2 * LANES)

    full = np.stack([ordered(plain, mirror), ordered(plain, none), ordered(none, plain)])
    high = full.astype(jnp.bfloat16)
    low = (full - high.astype(np.float64)).astype(jnp.bfloat16)
    return np.stack([high, low], axis=1)


def channelize_kernel(volt_ref, halo_ref, window_ref, twiddle_ref, dft_ref, out_ref, late, inner):
    inputs = volt_ref.shape[0]
    spectra = volt_ref.shape[1] // NFFT
    late[...] = halo_ref[...].astype(jnp.float32)

    def filter_rows(group, carry):
        first = pl.multiple_of(group * 8, 8)
        at = pl.ds(first, 8)
        for s in range(spectra):
            pieces = []
            for a in range(RADIX):
                total = None
                for tap in range(TAPS):
                    block = s + tap
                    if block < spectra:
                        col = block * NFFT + a * LANES
                        sample = volt_ref[at, col : col + LANES].astype(jnp.float32)
                    else:
                        col = (block - spectra) * NFFT + a * LANES
                        sample = late[at, col : col + LANES]
                    term = window_ref[tap, :, a * LANES : (a + 1) * LANES] * sample
                    total = term if total is None else total + term
                pieces.append(total)
            to = pl.ds(pl.multiple_of(s * inputs + first, 8), 8)
            for k, (re, im) in enumerate(real_dft(pieces)):
                cos, sin = twiddle_ref[k, 0], twiddle_ref[k, 1]
                if im is None:
                    inner[k, to, :LANES] = re * cos
                    inner[k, to, LANES:] = -re * sin
                else:
                    inner[k, to, :LANES] = re * cos + im * sin
                    inner[k, to, LANES:] = im * cos - re * sin
        return carry

    lax.fori_loop(0, inputs // 8, filter_rows, 0)

    def product(which, bins):
        over = (((1,), (1,)), ((), ()))
        dot = functools.partial(
            lax.dot_general, dimension_numbers=over, preferred_element_type=jnp.float32
        )
        high = bins.astype(jnp.bfloat16)
        low = (bins - high.astype(jnp.float32)).astype(jnp.bfloat16)
        return dot(dft_ref[which, 0], high) + (
            dot(dft_ref[which, 1], high) + dot(dft_ref[which, 0], low)
        )

    def put(k, value):
        groups, _, size, lanes = out_ref.shape
        out_ref[:, k] = value.astype(jnp.bfloat16).reshape(groups, size, lanes)

    put(0, product(1, inner[0]) + product(2, inner[RADIX // 2]))

    def transform_bin(k, carry):
        put(k, product(0, inner[k]))
        return carry

    lax.fori_loop(1, RADIX // 2, transform_bin, 0)


def channelize(voltages, halo, groups):
    inputs = voltages.shape[0]
    rows = inputs * (voltages.shape[1] // NFFT)
    window = jnp.broadcast_to(pfb_window()[:, None, :], (TAPS, 8, NFFT))
    return pl.pallas_call(
        channelize_kernel,
        out_shape=jax.ShapeDtypeStruct(
            (groups, RADIX // 2, 2 * LANES // groups, rows), jnp.bfloat16
        ),
        scratch_shapes=[
            pltpu.VMEM(halo.shape, jnp.float32),
            pltpu.VMEM((RADIX // 2 + 1, rows, 2 * LANES), jnp.float32),
        ],
        name="channelize",
    )(voltages, halo, window, twiddles(), second_stage(groups))


def window_table():
    total_len = TAPS * NFFT
    pos = np.arange(total_len, dtype=np.float64)
    taper_win = 0.5 - 0.5 * np.cos(2.0 * np.pi * (pos + 0.5) / total_len)
    coeffs = np.sinc((pos - total_len / 2 + 0.5) / NFFT) * taper_win
    coeffs = coeffs / np.sqrt(np.sum(coeffs * coeffs))
    return coeffs.reshape(TAPS, RADIX, LANES).astype(np.float32)


def twiddle_table():
    angle = 2.0 * np.pi * np.outer(np.arange(RADIX // 2 + 1), np.arange(LANES)) / NFFT
    return np.stack([np.cos(angle), np.sin(angle)], axis=1).astype(np.float32)


MESH = pl.DeviceIdType.MESH
HALO = TAPS - 1
PAIRS = RADIX // 4
LATE = 2
CHUNKS = 4


def spectra_kernel(
    volt_ref, window_ref, twiddle_ref, dft_ref, gain_ref, cal_ref,
    blocks, win, turn, filtered, inner, inner_last, send, recv, rows_buf,
    halo_send, halo_recv, send_sems, early_sem, late_sems,
):
    tm_count, chan_count = lax.axis_size("tm"), lax.axis_size("chan")
    tm, chan = lax.axis_index("tm"), lax.axis_index("chan")
    inputs = volt_ref.shape[0]
    spec_dev = volt_ref.shape[1] // NFFT
    slots = send.shape[0]
    devices = tm_count * chan_count
    last = tm_count - 1

    barrier = pltpu.get_barrier_semaphore()
    for tm_step in range(tm_count):
        for chan_step in range(chan_count):
            if tm_step or chan_step:
                peer = {
                    "tm": lax.rem(tm + tm_step, tm_count),
                    "chan": lax.rem(chan + chan_step, chan_count),
                }
                pl.semaphore_signal(barrier, inc=1, device_id=peer, device_id_type=MESH)

    def load_block(b):
        def column(a, carry):
            col = pl.multiple_of(b * NFFT + a * LANES, LANES)
            blocks[HALO + b, a] = (
                volt_ref[:, pl.ds(col, LANES)].astype(jnp.float32).astype(jnp.bfloat16)
            )
            return carry

        lax.fori_loop(0, RADIX, column, 0)

    def halo_copy(h):
        return pltpu.make_async_remote_copy(
            src_ref=blocks.at[spec_dev + h],
            dst_ref=blocks.at[h],
            send_sem=halo_send.at[h],
            recv_sem=halo_recv.at[h],
            device_id={"tm": jnp.minimum(tm + 1, last)},
            device_id_type=MESH,
        )

    for h in reversed(range(HALO)):
        load_block(spec_dev - HALO + h)

    pl.semaphore_wait(barrier, devices - 1)

    @pl.when(tm < last)
    def _():
        for h in reversed(range(HALO)):
            halo_copy(h).start()

    for b in range(spec_dev - HALO):
        load_block(b)

    @pl.when(tm == last)
    def _():
        def clear(a, carry):
            for b in range(HALO):
                blocks[HALO + spec_dev + b, a] = jnp.zeros((inputs, LANES), jnp.bfloat16)
            return carry

        lax.fori_loop(0, RADIX, clear, 0)

    def spread(a, carry):
        for tap in range(TAPS):
            win[tap, a] = jnp.broadcast_to(window_ref[tap, pl.ds(a, 1), :], (8, LANES))
        return carry

    lax.fori_loop(0, RADIX, spread, 0)
    for k in range(RADIX // 2 + 1):
        for part in range(2):
            turn[k, part] = jnp.broadcast_to(twiddle_ref[k, part : part + 1, :], (8, LANES))

    def product(which, bins):
        over = (((1,), (1,)), ((), ()))
        dot = functools.partial(
            lax.dot_general, dimension_numbers=over, preferred_element_type=jnp.float32
        )
        high = bins.astype(jnp.bfloat16)
        low = (bins - high.astype(jnp.float32)).astype(jnp.bfloat16)
        return dot(dft_ref[which, 0], high) + (
            dot(dft_ref[which, 1], high) + dot(dft_ref[which, 0], low)
        )

    def transform(slot):
        def filter_column(a, carry):
            taps = [win[tap, a] for tap in range(TAPS)]
            for row in range(0, inputs, 16):
                total = None
                for tap in range(TAPS):
                    sample = blocks[slot + tap, a, row : row + 16].astype(jnp.float32)
                    term = taps[tap][None] * sample.reshape(2, 8, LANES)
                    total = term if total is None else total + term
                filtered[a, row : row + 16] = total.reshape(16, LANES)
            return carry

        lax.fori_loop(0, RADIX, filter_column, 0)

        def first_stage(group, carry):
            at = pl.ds(pl.multiple_of(group * 8, 8), 8)
            upper = pl.ds(pl.multiple_of(inputs + group * 8, 8), 8)
            pieces = [filtered[a, at] for a in range(RADIX)]
            for k, (re, im) in enumerate(real_dft(pieces)):
                cos, sin = turn[k, 0], turn[k, 1]
                if im is None:
                    o_re, o_im = re * cos, -re * sin
                else:
                    o_re, o_im = re * cos + im * sin, im * cos - re * sin
                if k == RADIX // 2:
                    inner_last[at, :LANES] = o_re
                    inner_last[at, LANES:] = o_im
                else:
                    rows = at if k < PAIRS else upper
                    inner[k % PAIRS, rows, :LANES] = o_re
                    inner[k % PAIRS, rows, LANES:] = o_im
            return carry

        lax.fori_loop(0, inputs // 8, first_stage, 0)

        def put(pair, value):
            send[slot, :, pair] = value.astype(jnp.bfloat16).reshape(devices, -1, LANES)

        first = product(1, inner[0, :inputs]) + product(2, inner_last[...])
        put(0, jnp.concatenate([first, product(0, inner[0, inputs:])], axis=1))

        def second(pair, carry):
            put(pair, product(0, inner[pair]))
            return carry

        lax.fori_loop(1, PAIRS, second, 0)

    def deliver(slot, pairs, sem):
        at = spec_dev * tm - HALO + slot
        for i in range(tm_count):
            peer_tm = jnp.where(2 * tm >= tm_count, i, last - i)
            for step in range(chan_count):
                peer_chan = lax.rem(chan + step, chan_count)
                src = send.at[slot, peer_tm * chan_count + peer_chan, pairs]
                dst = recv.at[chan, at, pairs]

                def remote(src=src, dst=dst, peer_tm=peer_tm, peer_chan=peer_chan):
                    pltpu.make_async_remote_copy(
                        src_ref=src,
                        dst_ref=dst,
                        send_sem=send_sems.at[slot],
                        recv_sem=sem,
                        device_id={"tm": peer_tm, "chan": peer_chan},
                        device_id_type=MESH,
                    ).start()

                if step:
                    remote()
                else:
                    pl.when(peer_tm != tm)(remote)

                    @pl.when(peer_tm == tm)
                    def _(src=src, dst=dst):
                        pltpu.make_async_copy(src, dst, sem).start()

    def run(slot):
        transform(slot)

        @pl.when(slot >= LATE)
        def _():
            deliver(slot, pl.ds(0, PAIRS), early_sem)

    def forward(step, carry):
        slot = step + HALO

        @pl.when(jnp.logical_or(slot < spec_dev, tm == last))
        def _():
            run(slot)

        return carry

    lax.fori_loop(0, spec_dev, forward, 0)

    def backward(step, carry):
        slot = HALO - 1 - step

        @pl.when(tm > 0)
        def _():
            halo_copy(slot).wait_recv()
            run(slot)

        return carry

    lax.fori_loop(0, HALO, backward, 0)

    size = PAIRS // CHUNKS

    @pl.when(tm > 0)
    def _():
        def piece(chunk, carry):
            for slot in reversed(range(LATE)):
                deliver(slot, pl.ds(chunk * size, size), late_sems.at[chunk])
            return carry

        lax.fori_loop(0, CHUNKS, piece, 0)

    late = LATE * last
    early = tm_count * spec_dev - late

    def drain(ref, sem):
        pltpu.make_async_copy(ref, ref, sem).wait()

    drain(recv.at[:, pl.ds(0, early)], early_sem)

    spectra = tm_count * spec_dev
    rows = 2 * LANES // devices
    block = rows // 4

    def calibrate(chunk, carry):
        drain(recv.at[:, pl.ds(0, late), pl.ds(chunk * size, size)], late_sems.at[chunk])
        for part in range(size):
            pair = chunk * size + part
            for c in range(chan_count):
                rows_buf[c] = recv[c, :, pair].astype(jnp.float32).reshape(spectra * rows, LANES)
            for mirror in range(2):
                for q in range(block):
                    row = 2 * block * mirror + q
                    pick = lambda r: [
                        rows_buf[c, pl.ds(r, spectra, stride=rows), :] for c in range(chan_count)
                    ]
                    all_re, all_im = pick(row), pick(row + block)
                    for half in range(2):
                        cols = slice(half * inputs, (half + 1) * inputs)
                        a_re = jnp.concatenate([v[:, cols] for v in all_re], axis=1)
                        a_im = jnp.concatenate([v[:, cols] for v in all_im], axis=1)
                        k = pair + half * PAIRS
                        if mirror:
                            k = jnp.where(k == 0, RADIX // 2, RADIX - k)
                        channel = q * RADIX + k
                        g_re = gain_ref[0, pl.ds(channel, 1), :]
                        g_im = gain_ref[1, pl.ds(channel, 1), :]
                        cal_re = (g_re * a_re - g_im * a_im).astype(jnp.bfloat16)
                        cal_im = (g_re * a_im + g_im * a_re).astype(jnp.bfloat16)
                        cal_ref[channel, :spectra] = cal_re
                        cal_ref[channel, spectra:] = cal_im
        return carry

    lax.fori_loop(0, CHUNKS, calibrate, 0)

    @pl.when(tm < last)
    def _():
        for h in range(HALO):
            halo_copy(h).wait_send()

    for slot in range(slots):

        def sent(slot=slot):
            drain(send.at[slot, pl.ds(0, devices - 1)], send_sems.at[slot])

        if slot < HALO:
            pl.when(tm > 0)(sent)
        elif slot < spec_dev:
            sent()
        else:
            pl.when(tm == last)(sent)


def channel_spectra(voltages, cal_gains, tm_count, chan_count):
    inputs = voltages.shape[0]
    spec_dev = voltages.shape[1] // NFFT
    spectra = spec_dev * tm_count
    devices = tm_count * chan_count
    slots = spec_dev + HALO
    _, chan_local, all_inputs = cal_gains.shape
    rows = 2 * LANES // devices
    return pl.pallas_call(
        spectra_kernel,
        out_shape=jax.ShapeDtypeStruct((chan_local, 2 * spectra, all_inputs), jnp.bfloat16),
        scratch_shapes=[
            pltpu.VMEM((spec_dev + 2 * HALO, RADIX, inputs, LANES), jnp.bfloat16),
            pltpu.VMEM((TAPS, RADIX, 8, LANES), jnp.float32),
            pltpu.VMEM((RADIX // 2 + 1, 2, 8, LANES), jnp.float32),
            pltpu.VMEM((RADIX, inputs, LANES), jnp.float32),
            pltpu.VMEM((PAIRS, 2 * inputs, 2 * LANES), jnp.float32),
            pltpu.VMEM((inputs, 2 * LANES), jnp.float32),
            pltpu.VMEM((slots, devices, PAIRS, rows, LANES), jnp.bfloat16),
            pltpu.VMEM((chan_count, spectra, PAIRS, rows, LANES), jnp.bfloat16),
            pltpu.VMEM((chan_count, spectra * rows, LANES), jnp.float32),
            pltpu.SemaphoreType.DMA((HALO,)),
            pltpu.SemaphoreType.DMA((HALO,)),
            pltpu.SemaphoreType.DMA((slots,)),
            pltpu.SemaphoreType.DMA,
            pltpu.SemaphoreType.DMA((CHUNKS,)),
        ],
        compiler_params=pltpu.CompilerParams(collective_id=0, has_side_effects=True),
        name="spectra",
    )(voltages, window_table(), twiddle_table(), second_stage(devices), cal_gains)


def correlate_kernel(
    spec_ref, gain_ref, delay_ref, vis_ref, power_ref, cur_re, cur_im, rot_re, rot_im, w_re, w_im
):
    step = pl.program_id(0)
    block = spec_ref.shape[1]
    spectra = spec_ref.shape[2]
    inputs = spec_ref.shape[3]
    beams = delay_ref.shape[0]

    @pl.when(step == 0)
    def _():
        chan_count = lax.axis_size("chan")
        first = (lax.axis_index("tm") * chan_count + lax.axis_index("chan")) * (
            block * pl.num_programs(0)
        )
        delays = delay_ref[...].T
        start = (delays * first % NFFT).astype(jnp.float32) * (2.0 * math.pi / NFFT)
        turn = delays.astype(jnp.float32) * (2.0 * math.pi / NFFT)
        norm = 1.0 / math.sqrt(inputs)
        cur_re[...] = jnp.cos(start) * norm
        cur_im[...] = -jnp.sin(start) * norm
        rot_re[...] = jnp.cos(turn)
        rot_im[...] = -jnp.sin(turn)

    rows = 16

    def advance(chunk, carry):
        at = pl.ds(pl.multiple_of(chunk * rows, rows), rows)
        c_re, c_im = cur_re[at, :], cur_im[at, :]
        r_re, r_im = rot_re[at, :], rot_im[at, :]
        for c in range(block):
            w_re[c, at, :] = c_re.astype(jnp.bfloat16)
            w_im[c, at, :] = c_im.astype(jnp.bfloat16)
            c_re, c_im = c_re * r_re - c_im * r_im, c_re * r_im + c_im * r_re
        cur_re[at, :] = c_re
        cur_im[at, :] = c_im
        return carry

    lax.fori_loop(0, inputs // rows, advance, 0, unroll=True)

    for c in range(block):
        a_re = spec_ref[0, c].astype(jnp.float32)
        a_im = spec_ref[1, c].astype(jnp.float32)
        g_re = gain_ref[0, c : c + 1, :]
        g_im = gain_ref[1, c : c + 1, :]
        cal_re = (g_re * a_re - g_im * a_im).astype(jnp.bfloat16)
        cal_im = (g_re * a_im + g_im * a_re).astype(jnp.bfloat16)
        stacked = jnp.concatenate([cal_re, cal_im], axis=0)
        flipped = jnp.concatenate([cal_im, -cal_re], axis=0)
        over_time = (((0,), (0,)), ((), ()))
        for part, left in enumerate((stacked, flipped)):
            vis = lax.dot_general(left, stacked, over_time, preferred_element_type=jnp.float32)
            vis_ref[part, c] = (vis * (1.0 / spectra)).astype(jnp.bfloat16)
        by_re = jnp.dot(stacked, w_re[c], preferred_element_type=jnp.float32)
        by_im = jnp.dot(stacked, w_im[c], preferred_element_type=jnp.float32)
        beam_re = by_re[:spectra] - by_im[spectra:]
        beam_im = by_re[spectra:] + by_im[:spectra]
        power_ref[c] = (beam_re * beam_re + beam_im * beam_im).astype(jnp.bfloat16)


def correlate(spectra, beam_delays, cal_gains):
    _, chan_local, spectra_total, inputs = spectra.shape
    beams = beam_delays.shape[0]
    block = math.gcd(chan_local, 8)
    table = pltpu.VMEM((inputs, beams), jnp.float32)
    return pl.pallas_call(
        correlate_kernel,
        grid=(chan_local // block,),
        in_specs=[
            pl.BlockSpec((2, block, spectra_total, inputs), lambda g: (0, g, 0, 0)),
            pl.BlockSpec((2, block, inputs), lambda g: (0, g, 0)),
            pl.BlockSpec((beams, inputs), lambda g: (0, 0)),
        ],
        out_specs=[
            pl.BlockSpec((2, block, inputs, inputs), lambda g: (0, g, 0, 0)),
            pl.BlockSpec((block, spectra_total, beams), lambda g: (g, 0, 0)),
        ],
        out_shape=[
            jax.ShapeDtypeStruct((2, chan_local, inputs, inputs), jnp.bfloat16),
            jax.ShapeDtypeStruct((chan_local, spectra_total, beams), jnp.bfloat16),
        ],
        scratch_shapes=[table] * 4 + [pltpu.VMEM((block, inputs, beams), jnp.bfloat16)] * 2,
        compiler_params=pltpu.CompilerParams(dimension_semantics=("arbitrary",)),
        name="correlate",
    )(spectra, cal_gains, beam_delays)


def beams_kernel(
    cal_ref, delay_ref, vis_ref, power_ref, cur_re, cur_im, rot_re, rot_im, w_re, w_im
):
    step = pl.program_id(0)
    block = cal_ref.shape[0]
    spectra = cal_ref.shape[1] // 2
    inputs = cal_ref.shape[2]
    beams = delay_ref.shape[0]

    @pl.when(step == 0)
    def _():
        chan_count = lax.axis_size("chan")
        first = (lax.axis_index("tm") * chan_count + lax.axis_index("chan")) * (
            block * pl.num_programs(0)
        )
        delays = delay_ref[...].T
        start = (delays * first % NFFT).astype(jnp.float32) * (2.0 * math.pi / NFFT)
        turn = delays.astype(jnp.float32) * (2.0 * math.pi / NFFT)
        norm = 1.0 / math.sqrt(inputs)
        cur_re[...] = jnp.cos(start) * norm
        cur_im[...] = -jnp.sin(start) * norm
        rot_re[...] = jnp.cos(turn)
        rot_im[...] = -jnp.sin(turn)

    rows = 16

    def advance(chunk, carry):
        at = pl.ds(pl.multiple_of(chunk * rows, rows), rows)
        c_re, c_im = cur_re[at, :], cur_im[at, :]
        r_re, r_im = rot_re[at, :], rot_im[at, :]
        for c in range(block):
            w_re[c, at, :] = c_re.astype(jnp.bfloat16)
            w_im[c, at, :] = c_im.astype(jnp.bfloat16)
            c_re, c_im = c_re * r_re - c_im * r_im, c_re * r_im + c_im * r_re
        cur_re[at, :] = c_re
        cur_im[at, :] = c_im
        return carry

    lax.fori_loop(0, inputs // rows, advance, 0, unroll=True)

    for c in range(block):
        cal_re, cal_im = cal_ref[c, :spectra], cal_ref[c, spectra:]
        stacked = jnp.concatenate([cal_re, cal_im], axis=0)
        flipped = jnp.concatenate([cal_im, -cal_re], axis=0)
        over_time = (((0,), (0,)), ((), ()))
        for part, left in enumerate((stacked, flipped)):
            vis = lax.dot_general(left, stacked, over_time, preferred_element_type=jnp.float32)
            vis_ref[part, c] = (vis * (1.0 / spectra)).astype(jnp.bfloat16)
        by_re = jnp.dot(stacked, w_re[c], preferred_element_type=jnp.float32)
        by_im = jnp.dot(stacked, w_im[c], preferred_element_type=jnp.float32)
        beam_re = by_re[:spectra] - by_im[spectra:]
        beam_im = by_re[spectra:] + by_im[:spectra]
        power_ref[c] = (beam_re * beam_re + beam_im * beam_im).astype(jnp.bfloat16)


def beams_and_visibilities(calibrated, beam_delays):
    chan_local, rows, inputs = calibrated.shape
    spectra_total = rows // 2
    beams = beam_delays.shape[0]
    block = math.gcd(chan_local, 8)
    table = pltpu.VMEM((inputs, beams), jnp.float32)
    return pl.pallas_call(
        beams_kernel,
        grid=(chan_local // block,),
        in_specs=[
            pl.BlockSpec((block, rows, inputs), lambda g: (g, 0, 0)),
            pl.BlockSpec((beams, inputs), lambda g: (0, 0)),
        ],
        out_specs=[
            pl.BlockSpec((2, block, inputs, inputs), lambda g: (0, g, 0, 0)),
            pl.BlockSpec((block, spectra_total, beams), lambda g: (g, 0, 0)),
        ],
        out_shape=[
            jax.ShapeDtypeStruct((2, chan_local, inputs, inputs), jnp.bfloat16),
            jax.ShapeDtypeStruct((chan_local, spectra_total, beams), jnp.bfloat16),
        ],
        scratch_shapes=[table] * 4 + [pltpu.VMEM((block, inputs, beams), jnp.bfloat16)] * 2,
        compiler_params=pltpu.CompilerParams(dimension_semantics=("arbitrary",)),
        name="beams",
    )(calibrated, beam_delays)


def shards(voltages, beam_delays, cal_gains):
    inp_dev = voltages.shape[0]
    spec_dev = voltages.shape[1] // NFFT
    tm_count = lax.axis_size("tm")
    chan_count = lax.axis_size("chan")
    spectra_total = spec_dev * tm_count
    devices = tm_count * chan_count
    if 2 * inp_dev == LANES and spec_dev >= HALO and tm_count > 1 and 2 * LANES == 16 * devices:
        calibrated = channel_spectra(voltages, cal_gains, tm_count, chan_count)
        return beams_and_visibilities(calibrated, beam_delays)
    halo = shifted(voltages[:, : (TAPS - 1) * NFFT].astype(jnp.bfloat16), "tm", -1)
    half = LANES // 2
    bins = channelize(voltages, halo, half).reshape(RADIX // 2, half, 2, 2, spec_dev, inp_dev)
    plain, mirror = bins[:, :, 0], bins[:, :, 1]
    bins = jnp.concatenate([plain, mirror[:1], mirror[:0:-1]], axis=0)
    packed = bins.transpose(2, 1, 0, 3, 4).reshape(2, CH, spec_dev, inp_dev)
    chan_local = CH // (tm_count * chan_count)
    reordered = packed.reshape(2, tm_count, chan_count, chan_local, spec_dev, inp_dev)
    reordered = reordered.transpose(0, 2, 1, 3, 4, 5).reshape(2, CH, spec_dev, inp_dev)
    sectioned = lax.all_to_all(reordered, "chan", split_axis=1, concat_axis=3, tiled=True)
    turned = lax.all_to_all(sectioned, "tm", split_axis=1, concat_axis=2, tiled=True)
    return correlate(turned, beam_delays, cal_gains)


def solution(mesh):
    return jax.shard_map(
        shards,
        mesh=mesh,
        in_specs=(P(("grp", "chan"), "tm"), P(), P(None, ("grp", "tm", "chan"), None)),
        out_specs=(
            P(None, ("grp", "tm", "chan"), None, None),
            P(("grp", "tm", "chan"), None, None),
        ),
        check_vma=False,
    )
```
